128 devices in a mesh: req: 32 (over y, x, core), mlp: 4 (over z).
Axes of the slice: x: 4, y: 4, z: 4, core: 2. Of those that a mesh axis runs over, the one named last changes fastest.
Arguments:
- tokens: bfloat16 [8192, 2560], P('req'), may hold values from -125 to 125
- lengths: int32 [32, 4], P('req'), may hold values from 1 to 128, 256 in all within a row
- page_table: int32 [32, 16], P('req'), may hold values from 0 to 15, each once within a row
- attn_norm: float32 [2560], replicated, may hold values from 0.25 to 1.75
- qkv_weight: bfloat16 [2560, 8, 768], P(None, 'mlp'), may hold values from -0.125 to 0.125
- q_norm: float32 [128], replicated, may hold values from 0.25 to 1.75
- k_norm: float32 [128], replicated, may hold values from 0.25 to 1.75
- o_weight: bfloat16 [4096, 2560], P('mlp'), may hold values from -0.09375 to 0.09375
- mlp_norm: float32 [2560], replicated, may hold values from 0.25 to 1.75
- gate_up: bfloat16 [9728, 2, 2560], P(('req', 'mlp')), may hold values from -0.125 to 0.125
- down_weight: bfloat16 [9728, 2560], P(('req', 'mlp')), may hold values from -0.0625 to 0.0625
Outputs:
- layer_out: bfloat16 [8192, 2560], P(('req', 'mlp'))
- kv_cache: bfloat16 [2, 512, 16, 8, 128], P(None, 'req', None, 'mlp')
The draws below stay inside these ranges and needn't reach their ends.
Inputs may be any that keep to these rules, and one draw needn't show every extreme that they name: `lengths`: each row sums to 256, and the longest prompt of every pack is exactly 128. `page_table`: each row is a permutation of 0 .. 15.
All inputs are finite; a program needn't handle non-finite values.
Results may differ from the reference program's by a relative error of at most 0.0049.
Values may be sent and summed in bfloat16 or wider, within the bound.
No kernel may reach another device: no remote copies, remote signals or barrier semaphores. Data moves between devices by JAX's collectives and lax.ppermute only.
A program may use at most 128 MiB of HBM per device.

```python
import math
import jax
import jax.numpy as jnp
import numpy as np
from jax import lax

D = 2560
H = 32
KV = 8
HD = 128
FF = 9728
SEQS = 4
PAGE = 16
GQ = 4
SLOTS = 256
LONGEST = 128
PAGES = 16
GROUPS = 32
TOKENS = 8192


def draw_tokens(key, part):
    key_base, key_rows, key_cols = jax.random.split(key, 3)
    row_scale = jnp.exp(jax.random.uniform(key_rows, (TOKENS, 1), jnp.float32, 0.0, math.log(10.0)))
    col_scale = jnp.exp(jax.random.uniform(key_cols, (1, D), jnp.float32, 0.0, math.log(10.0)))
    base = jnp.clip(jax.random.normal(key_base, (TOKENS, D), jnp.float32), -5.0, 5.0)
    return (base * row_scale * col_scale / 4.0).astype(jnp.bfloat16)


def level_of(stream_key, dims, cuts, smallest, top_value):
    level, own = 1.0, jax.random.fold_in(stream_key, 6)
    for dim, shards_of in cuts:
        heights = jnp.exp(jax.random.uniform(jax.random.fold_in(own, dim), (shards_of,), jnp.float32, smallest / len(cuts), top_value / len(cuts)))
        level = level * jnp.repeat(heights, dims[dim] // shards_of).reshape([-1 if axis == dim else 1 for axis in range(len(dims))])
    return level


def length_profile(count, total, limit, slope):
    portions = [(1 << 20) // math.isqrt(rank ** slope) + 1 for rank in range(2, count + 1)]
    rest, given = total - limit - (count - 1), [1] * (count - 1)
    while rest > 0:
        free = [i for i in range(count - 1) if given[i] < limit]
        mass, budget = sum([portions[i] for i in free]), rest
        for i in free:
            extra = min(limit - given[i], max(1, budget * portions[i] // mass), rest)
            given[i] = given[i] + extra
            rest = rest - extra
    return np.array([limit] + given)


def ragged(rng, count, total, most, lean):
    if count == 2:
        one = jax.random.randint(rng, (), max(1, total - most), min(most, total - 1) + 1)
        return jnp.stack([one, total - one])
    sizes = jnp.asarray(length_profile(count, total, most, lean), jnp.int32)
    twos = (count - 1) // 2
    giver, taker = sizes[1:1 + 2 * twos:2], sizes[2:2 + 2 * twos:2]
    slack = jnp.minimum(giver - 1, most - taker)
    moved = jax.random.randint(jax.random.fold_in(rng, 1), (twos,), 0, 1 << 20) % (slack + 1)
    sizes = sizes.at[1:1 + 2 * twos:2].set(giver - moved).at[2:2 + 2 * twos:2].set(taker + moved)
    return sizes[jax.random.permutation(jax.random.fold_in(rng, 2), count)]


def centred(stream_key, shape, spread, most, cuts=(), kind=jnp.bfloat16):
    result = spread * jax.random.normal(stream_key, shape, jnp.float32)
    if cuts:
        result = result * level_of(stream_key, shape, cuts, -0.22, 0.18)
    return jnp.clip(result, -most, most).astype(kind)


def setup_inputs(seed: int = 0) -> dict:
    splits = jax.random.split(jax.random.key(seed), 12)
    return {
        "tokens": draw_tokens(jax.random.fold_in(splits[11], 71), 0),
        "lengths": jax.vmap(lambda own: ragged(own, SEQS, SLOTS, LONGEST, 2))(jax.random.split(splits[1], GROUPS)).reshape((GROUPS, SEQS)).astype(jnp.int32),
        "page_table": jax.vmap(lambda own: jax.random.permutation(own, PAGES))(jax.random.split(splits[2], GROUPS)).reshape((GROUPS, PAGES)).astype(jnp.int32),
        "attn_norm": jnp.clip(1.0 + 0.15 * jax.random.normal(splits[3], (D,), jnp.float32), 0.25, 1.75),
        "qkv_weight": centred(splits[4], (D, KV, (GQ + 2) * HD), D ** -0.5, 0.125, ((1, 4),)),
        "q_norm": jnp.clip(1.0 + 0.15 * jax.random.normal(splits[5], (HD,), jnp.float32), 0.25, 1.75),
        "k_norm": jnp.clip(1.0 + 0.15 * jax.random.normal(splits[6], (HD,), jnp.float32), 0.25, 1.75),
        "o_weight": centred(splits[7], (H * HD, D), (H * HD) ** -0.5, 0.09375, ((0, 4),)),
        "mlp_norm": jnp.clip(1.0 + 0.15 * jax.random.normal(splits[8], (D,), jnp.float32), 0.25, 1.75),
        "gate_up": centred(splits[9], (FF, 2, D), D ** -0.5, 0.125, ((0, 128),)),
        "down_weight": centred(splits[10], (FF, D), FF ** -0.5, 0.0625, ((0, 128),)),
    }


rope_theta = 1000000.0
norm_eps = 1e-06

def rms_scale(values, gain):
    mean_sq = lax.optimization_barrier(jnp.mean(values * values, axis=-1, keepdims=True))
    return values * lax.rsqrt(mean_sq + norm_eps) * gain

def positions_of(lengths, slots):
    ends = jnp.cumsum(lengths).astype(jnp.int32)
    slot_ids = jnp.arange(slots, dtype=jnp.int32)
    passed = (ends[None, :] <= slot_ids[:, None]).astype(jnp.int32)
    segment = lax.optimization_barrier(jnp.sum(passed, axis=1)).astype(jnp.int32)
    start = lax.optimization_barrier(jnp.sum(passed * lengths[None, :], axis=1)).astype(jnp.int32)
    return (slot_ids, segment, slot_ids - start)

def rotate(values, position, head_dim):
    half = head_dim // 2
    freq = rope_theta ** (-(2.0 * jnp.arange(half, dtype=jnp.float32)) / head_dim)
    angle = position.astype(jnp.float32)[:, None] * freq[None, :]
    shape = (angle.shape[0],) + (1,) * (values.ndim - 2) + (half,)
    cosine = jnp.cos(angle).reshape(shape)
    sine = jnp.sin(angle).reshape(shape)
    first = values[..., :half]
    second = values[..., half:]
    return jnp.concatenate([first * cosine - second * sine, second * cosine + first * sine], axis=-1)

def reference(tokens, lengths, page_table, attn_norm, qkv_weight, q_norm, k_norm, o_weight, mlp_norm, gate_up, down_weight):
    packed = tokens.reshape(GROUPS, SLOTS, D)

    def one_group(items):
        rows, lens, pages = items
        slot_ids, segment, position = positions_of(lens, SLOTS)
        normed = rms_scale(rows.astype(jnp.float32), attn_norm).astype(jnp.bfloat16)
        qkv = jnp.dot(normed, qkv_weight.reshape(D, KV * (GQ + 2) * HD), preferred_element_type=jnp.float32)
        qkv = qkv.reshape(SLOTS, KV, (GQ + 2) * HD)
        query = qkv[:, :, :GQ * HD].reshape(SLOTS, KV, GQ, HD)
        key = qkv[:, :, GQ * HD:(GQ + 1) * HD]
        value = qkv[:, :, (GQ + 1) * HD:]
        query = rotate(rms_scale(query, q_norm), position, HD).astype(jnp.bfloat16)
        key = rotate(rms_scale(key, k_norm), position, HD).astype(jnp.bfloat16)
        value = value.astype(jnp.bfloat16)
        key_pages = key.reshape(PAGES, PAGE, KV, HD)
        value_pages = value.reshape(PAGES, PAGE, KV, HD)
        cache = jnp.zeros((2, PAGES, PAGE, KV, HD), jnp.bfloat16).at[:, pages].set(jnp.stack([key_pages, value_pages]))
        scores = jnp.einsum('skgd,tkd->kgst', query.astype(jnp.float32), key.astype(jnp.float32)) / math.sqrt(HD)
        allowed = (segment[:, None] == segment[None, :]) & (slot_ids[None, :] <= slot_ids[:, None])
        weights = jnp.where(allowed, jnp.exp(scores), 0.0)
        probs = (weights / lax.optimization_barrier(jnp.sum(weights, axis=-1, keepdims=True))).astype(jnp.bfloat16)
        context = jnp.einsum('kgst,tkd->skgd', probs.astype(jnp.float32), value.astype(jnp.float32))
        context = context.astype(jnp.bfloat16).reshape(SLOTS, H * HD)
        attn_out = jnp.dot(context, o_weight, preferred_element_type=jnp.float32)
        resid = rows.astype(jnp.float32) + attn_out
        mlp_in = rms_scale(resid, mlp_norm).astype(jnp.bfloat16)
        gate = jnp.dot(mlp_in, gate_up[:, 0, :].T, preferred_element_type=jnp.float32)
        upper = jnp.dot(mlp_in, gate_up[:, 1, :].T, preferred_element_type=jnp.float32)
        act = (jax.nn.silu(gate) * upper).astype(jnp.bfloat16)
        mlp_out = jnp.dot(act, down_weight, preferred_element_type=jnp.float32)
        return ((resid + mlp_out).astype(jnp.bfloat16), cache)
    outputs, caches = lax.map(one_group, (packed, lengths, page_table))
    layer_out = outputs.reshape(TOKENS, D)
    kv_cache = jnp.transpose(caches, (1, 0, 2, 3, 4, 5)).reshape(2, GROUPS * PAGES, PAGE, KV, HD)
    return (layer_out, kv_cache)
```

```python
import math

import jax
import jax.numpy as jnp
from jax import lax
from jax.sharding import PartitionSpec as P

rope_theta = 1000000.0
norm_eps = 1e-06

AXES = ("req", "mlp")

bf16 = jnp.bfloat16
f32 = jnp.float32

FLIPS = {
    "ya": (1, 0, 0, 0),
    "yb": (3, 0, 0, 0),
    "xa": (0, 1, 0, 0),
    "xb": (0, 3, 0, 0),
    "za": (0, 0, 0, 1),
    "zb": (0, 0, 0, 3),
    "core": (0, 0, 1, 0),
}
CUBE = ("ya", "za", "yb", "zb")


def pairs(flip_core0, flip_core1):
    out = []
    for y in range(4):
        for x in range(4):
            for core in range(2):
                for z in range(4):
                    fy, fx, fc, fz = FLIPS[flip_core1 if core else flip_core0]
                    there = (y ^ fy, x ^ fx, core ^ fc, z ^ fz)
                    src = ((y * 4 + x) * 2 + core) * 4 + z
                    dst = ((there[0] * 4 + there[1]) * 2 + there[2]) * 4 + there[3]
                    out.append((src, dst))
    return out


def send(values, flip_core0, flip_core1):
    return lax.ppermute(values, AXES, pairs(flip_core0, flip_core1))


def cube_send(values, slot, step):
    return send(values, CUBE[(slot + step) % 4], CUBE[(2 + slot + step) % 4])


def rms_scale(values, gain):
    mean_sq = jnp.mean(values * values, axis=-1, keepdims=True)
    return values * lax.rsqrt(mean_sq + norm_eps) * gain


def positions_of(lengths, slots):
    ends = jnp.cumsum(lengths)
    slot_ids = jnp.arange(slots, dtype=jnp.int32)
    passed = (ends[None, :] <= slot_ids[:, None]).astype(jnp.int32)
    segment = jnp.sum(passed, axis=1)
    start = jnp.sum(passed * lengths[None, :], axis=1)
    return (slot_ids, segment, slot_ids - start)


def rotate(values, position, head_dim):
    half = head_dim // 2
    freq = rope_theta ** (-(2.0 * jnp.arange(half, dtype=f32)) / head_dim)
    angle = position.astype(f32)[:, None] * freq[None, :]
    shape = (angle.shape[0],) + (1,) * (values.ndim - 2) + (half,)
    cosine = jnp.cos(angle).reshape(shape)
    sine = jnp.sin(angle).reshape(shape)
    first = values[..., :half]
    second = values[..., half:]
    return jnp.concatenate(
        [first * cosine - second * sine, second * cosine + first * sine], axis=-1
    )


def per_device(
    tokens,
    lengths,
    page_table,
    attn_norm,
    qkv_weight,
    q_norm,
    k_norm,
    o_weight,
    mlp_norm,
    gate_up,
    down_weight,
):
    slots = tokens.shape[0]
    width = tokens.shape[1]
    head_dim = q_norm.shape[0]
    local_kv = qkv_weight.shape[1]
    group_q = qkv_weight.shape[2] // head_dim - 2
    pages = page_table.shape[1]
    page_rows = slots // pages
    owned = slots // 4
    core = lax.axis_index("req") % 2
    z = lax.axis_index("mlp")

    units = gate_up.shape[0]
    padded = -(-units // 16) * 16
    pad = ((0, padded - units), (0, 0))
    own = jnp.concatenate(
        [jnp.pad(gate_up[:, 0, :], pad), jnp.pad(gate_up[:, 1, :], pad), jnp.pad(down_weight, pad)]
    )
    own1 = send(own, "xa", "xb")
    pair = jnp.concatenate([own, own1])
    pair1 = send(pair, "xb", "xa")
    parts = [pair, pair1, send(pair, "core", "core"), send(pair1, "core", "core")]
    shards = []
    for part in parts:
        shards.append(part[: 3 * padded])
        shards.append(part[3 * padded :])

    slot_ids, segment, position = positions_of(lengths[0], slots)
    normed = rms_scale(tokens.astype(f32), attn_norm).astype(bf16)
    qkv = jnp.einsum("sd,dkc->skc", normed, qkv_weight, preferred_element_type=f32)
    query = qkv[:, :, : group_q * head_dim].reshape(slots, local_kv, group_q, head_dim)
    key = qkv[:, :, group_q * head_dim : (group_q + 1) * head_dim]
    value = qkv[:, :, (group_q + 1) * head_dim :]
    query = rotate(rms_scale(query, q_norm), position, head_dim).astype(bf16)
    key = rotate(rms_scale(key, k_norm), position, head_dim).astype(bf16)
    value = value.astype(bf16)
    key_pages = key.reshape(pages, page_rows, local_kv, head_dim)
    value_pages = value.reshape(pages, page_rows, local_kv, head_dim)
    kv_cache = jnp.zeros((2, pages, page_rows, local_kv, head_dim), bf16)
    kv_cache = kv_cache.at[:, page_table[0]].set(jnp.stack([key_pages, value_pages]))
    scores = jnp.einsum("skgd,tkd->kgst", query, key, preferred_element_type=f32) / math.sqrt(
        head_dim
    )
    allowed = (segment[:, None] == segment[None, :]) & (slot_ids[None, :] <= slot_ids[:, None])
    weights = jnp.where(allowed, jnp.exp(scores), 0.0)
    probs = (weights / jnp.sum(weights, axis=-1, keepdims=True)).astype(bf16)
    context = jnp.einsum("kgst,tkd->skgd", probs, value, preferred_element_type=f32)
    context = context.astype(bf16).reshape(slots, local_kv * group_q * head_dim)

    first = jnp.where(core == 0, 1, 3)
    second = jnp.where(core == 0, 3, 1)

    def rows_of(values, owner):
        return lax.dynamic_slice_in_dim(values, owner * owned, owned, 0)

    leaving = jnp.concatenate([rows_of(context, z ^ first), rows_of(context, z ^ first ^ second)])
    staying = jnp.concatenate([rows_of(context, z), rows_of(context, z ^ second)])
    out_leaving = jnp.dot(leaving, o_weight, preferred_element_type=f32).astype(bf16)
    arrived = send(out_leaving, "za", "zb").astype(f32)
    out_staying = jnp.dot(staying, o_weight, preferred_element_type=f32) + arrived
    arrived = send(out_staying[owned:].astype(bf16), "zb", "za").astype(f32)
    attn_out = out_staying[:owned] + arrived
    resid = rows_of(tokens, z).astype(f32) + attn_out
    mlp_in = rms_scale(resid, mlp_norm).astype(bf16)

    gate_w = jnp.concatenate([s[:padded] for s in shards])
    upper_w = jnp.concatenate([s[padded : 2 * padded] for s in shards])
    down_w = jnp.concatenate([s[2 * padded :] for s in shards])

    def feed_forward(rows):
        gate = jnp.einsum("td,fd->tf", rows, gate_w, preferred_element_type=f32)
        upper = jnp.einsum("td,fd->tf", rows, upper_w, preferred_element_type=f32)
        act = (jax.nn.silu(gate) * upper).astype(bf16)
        return jnp.dot(act, down_w, preferred_element_type=f32)

    half = owned // 2
    held = [mlp_in[:half], mlp_in[half:]]
    for step in range(3):
        held = [jnp.concatenate([h, cube_send(h, i, step)]) for i, h in enumerate(held)]
    far = [cube_send(h, i, 3) for i, h in enumerate(held)]
    near_out = feed_forward(jnp.concatenate(held))
    rows = 8 * half
    near_out = [near_out[:rows], near_out[rows:]]
    far_out = [feed_forward(h).astype(bf16) for h in far]
    total = [n + cube_send(f, i, 3).astype(f32) for i, (n, f) in enumerate(zip(near_out, far_out))]
    for step in (2, 1, 0):
        rows //= 2
        total = [
            t[:rows] + cube_send(t[rows:].astype(bf16), i, step).astype(f32)
            for i, t in enumerate(total)
        ]
    layer_out = (resid + jnp.concatenate(total)).astype(bf16)
    return (layer_out, kv_cache)


def solution(mesh):
    return jax.shard_map(
        per_device,
        mesh=mesh,
        in_specs=(
            P("req", None),
            P("req", None),
            P("req", None),
            P(),
            P(None, "mlp", None),
            P(),
            P(),
            P("mlp", None),
            P(),
            P(("req", "mlp"), None, None),
            P(("req", "mlp"), None),
        ),
        out_specs=(P(("req", "mlp"), None), P(None, "req", None, "mlp", None)),
        check_vma=False,
    )
```

```python
import math

import jax
import jax.numpy as jnp
from jax import lax
from jax.experimental import pallas as pl
from jax.experimental.pallas import tpu as pltpu
from jax.sharding import PartitionSpec as P


rope_theta = 1000000.0
norm_eps = 1e-06

AXES = ("req", "mlp")

bf16 = jnp.bfloat16
f32 = jnp.float32
VMEM_LIMIT = 16 * 2**20
INTERPRET = False
WHOLE = pl.BlockSpec(memory_space=pltpu.VMEM)

FLIPS = {
    "ya": (1, 0, 0, 0),
    "yb": (3, 0, 0, 0),
    "xa": (0, 1, 0, 0),
    "xb": (0, 3, 0, 0),
    "za": (0, 0, 0, 1),
    "zb": (0, 0, 0, 3),
    "core": (0, 0, 1, 0),
}
CUBE = ("ya", "za", "yb", "zb")


def pairs(flip_core0, flip_core1):
    out = []
    for y in range(4):
        for x in range(4):
            for core in range(2):
                for z in range(4):
                    fy, fx, fc, fz = FLIPS[flip_core1 if core else flip_core0]
                    there = (y ^ fy, x ^ fx, core ^ fc, z ^ fz)
                    src = ((y * 4 + x) * 2 + core) * 4 + z
                    dst = ((there[0] * 4 + there[1]) * 2 + there[2]) * 4 + there[3]
                    out.append((src, dst))
    return out


def send(values, flip_core0, flip_core1):
    return lax.ppermute(values, AXES, pairs(flip_core0, flip_core1))


def cube_send(values, slot, step):
    return send(values, CUBE[(slot + step) % 4], CUBE[(2 + slot + step) % 4])


def rms_scale(values, gain):
    mean_sq = jnp.mean(values * values, axis=-1, keepdims=True)
    return values * lax.rsqrt(mean_sq + norm_eps) * gain


def attention(qkv, q_norm, k_norm, lengths, page_table, place):
    local_kv, slots, _ = qkv.shape
    head_dim = q_norm.shape[0]
    half = head_dim // 2
    group_q = qkv.shape[2] // head_dim - 2
    prompts = lengths.shape[1]
    pages = page_table.shape[1]
    page_rows = slots // pages
    owned = slots // 4
    freq = rope_theta ** (-(2.0 * jnp.arange(half, dtype=f32)) / head_dim)
    freq = jnp.concatenate([freq, freq])[None, :]

    def kernel(lengths_ref, pages_ref, place_ref, qkv_ref, q_ref, k_ref, freq_ref, ctx_ref, kv_ref):
        def segments(dim, shape):
            ids = lax.broadcasted_iota(jnp.int32, shape, dim)
            segment = jnp.zeros(shape, jnp.int32)
            start = jnp.zeros(shape, jnp.int32)
            end = jnp.int32(0)
            for p in range(prompts):
                end = end + lengths_ref[0, p]
                segment = segment + (ids >= end).astype(jnp.int32)
                start = jnp.where(ids >= end, end, start)
            return ids, segment, ids - start

        _, _, position = segments(0, (slots, head_dim))
        angle = position.astype(f32) * freq_ref[...]
        cosine = jnp.cos(angle)
        sine = jnp.sin(angle)
        lane = lax.broadcasted_iota(jnp.int32, (slots, head_dim), 1)
        sine = jnp.where(lane < half, -sine, sine)
        query_id, query_segment, _ = segments(0, (slots, slots))
        key_id, key_segment, _ = segments(1, (slots, slots))
        allowed = (query_segment == key_segment) & (key_id <= query_id)

        def headed(values, gain):
            mean_sq = jnp.mean(values * values, axis=-1, keepdims=True)
            values = values * lax.rsqrt(mean_sq + norm_eps) * gain
            return (values * cosine + pltpu.roll(values, half, 1) * sine).astype(bf16)

        def block_at(owner):
            apart = owner ^ place_ref[0, 0]
            at = jnp.where(apart == place_ref[0, 1], 0, 1)
            at = jnp.where(apart == 0, 2, at)
            at = jnp.where(apart == place_ref[0, 2], 3, at)
            return pl.multiple_of(at * owned, owned)

        targets = [block_at(owner) for owner in range(4)]
        homes = [pl.multiple_of(pages_ref[0, p] * page_rows, page_rows) for p in range(pages)]
        for j in range(local_kv):
            key = headed(qkv_ref[j, :, group_q * head_dim : (group_q + 1) * head_dim], k_ref[...])
            value = qkv_ref[j, :, (group_q + 1) * head_dim :].astype(bf16)
            for p in range(pages):
                kv_ref[0, j, pl.ds(homes[p], page_rows), :] = key[p * page_rows : (p + 1) * page_rows]
                kv_ref[1, j, pl.ds(homes[p], page_rows), :] = value[
                    p * page_rows : (p + 1) * page_rows
                ]
            for i in range(group_q):
                query = headed(qkv_ref[j, :, i * head_dim : (i + 1) * head_dim], q_ref[...])
                scores = lax.dot_general(
                    query, key, (((1,), (1,)), ((), ())), preferred_element_type=f32
                ) * (1.0 / math.sqrt(head_dim))
                weights = jnp.where(allowed, jnp.exp(scores), 0.0)
                probs = (weights / jnp.sum(weights, axis=-1, keepdims=True)).astype(bf16)
                context = jnp.dot(probs, value, preferred_element_type=f32).astype(bf16)
                at = (j * group_q + i) * head_dim
                for owner in range(4):
                    ctx_ref[pl.ds(targets[owner], owned), at : at + head_dim] = context[
                        owner * owned : (owner + 1) * owned
                    ]

    scalars = pl.BlockSpec(memory_space=pltpu.SMEM)
    return pl.pallas_call(
        kernel,
        out_shape=[
            jax.ShapeDtypeStruct((slots, local_kv * group_q * head_dim), bf16),
            jax.ShapeDtypeStruct((2, local_kv, slots, head_dim), bf16),
        ],
        in_specs=[scalars] * 3 + [WHOLE] * 4,
        out_specs=[WHOLE] * 2,
        compiler_params=pltpu.CompilerParams(vmem_limit_bytes=VMEM_LIMIT),
        interpret=INTERPRET,
    )(lengths, page_table, place, qkv, q_norm[None, :], k_norm[None, :], freq)


def starts_of(pieces):
    return [sum(p.shape[0] for p in pieces[:i]) for i in range(len(pieces) + 1)]


def feed_forward_body(ins, rows, gate_upper_ref, down_ref, outs):
    starts = starts_of(ins)
    units = down_ref.shape[0]
    for i, piece in enumerate(ins):
        rows[starts[i] : starts[i + 1], :] = piece[...]
    hidden = lax.dot_general(
        rows[...], gate_upper_ref[...], (((1,), (1,)), ((), ())), preferred_element_type=f32
    )
    gate, upper = hidden[:, :units], hidden[:, units:]
    act = (gate / (1.0 + jnp.exp(-gate)) * upper).astype(bf16)
    out = jnp.dot(act, down_ref[...], preferred_element_type=f32)
    for i, piece in enumerate(outs):
        piece[...] = out[starts[i] : starts[i + 1], :].astype(piece.dtype)


def feed_forward(pieces, gate_upper, down, out_types):
    count = len(pieces)

    def kernel(*refs):
        feed_forward_body(
            refs[:count], refs[-1], refs[count], refs[count + 1], refs[count + 2 : -1]
        )

    return pl.pallas_call(
        kernel,
        out_shape=[jax.ShapeDtypeStruct(p.shape, t) for p, t in zip(pieces, out_types)],
        in_specs=[WHOLE] * (count + 2),
        out_specs=[WHOLE] * count,
        scratch_shapes=[pltpu.VMEM((starts_of(pieces)[-1], down.shape[1]), bf16)],
        compiler_params=pltpu.CompilerParams(vmem_limit_bytes=VMEM_LIMIT),
        interpret=INTERPRET,
    )(*pieces, gate_upper, down)


def feed_forward_first(pieces, shards, out_types):
    count, parts = len(pieces), len(shards)
    each = shards[0].shape[0] // 3
    width = shards[0].shape[1]
    units = parts * each

    def kernel(*refs):
        ins, held, outs = refs[:count], refs[count : count + parts], refs[count + parts : -3]
        gate_upper_ref, down_ref, rows = refs[-3:]
        for i, shard in enumerate(held):
            gate_upper_ref[i * each : (i + 1) * each, :] = shard[:each, :]
            gate_upper_ref[units + i * each : units + (i + 1) * each, :] = shard[each : 2 * each, :]
            down_ref[i * each : (i + 1) * each, :] = shard[2 * each :, :]
        feed_forward_body(ins, rows, gate_upper_ref, down_ref, outs)

    shapes = [jax.ShapeDtypeStruct(p.shape, t) for p, t in zip(pieces, out_types)]
    shapes.append(jax.ShapeDtypeStruct((2 * units, width), bf16))
    shapes.append(jax.ShapeDtypeStruct((units, width), bf16))
    outs = pl.pallas_call(
        kernel,
        out_shape=shapes,
        in_specs=[WHOLE] * (count + parts),
        out_specs=[WHOLE] * (count + 2),
        scratch_shapes=[pltpu.VMEM((starts_of(pieces)[-1], width), bf16)],
        compiler_params=pltpu.CompilerParams(vmem_limit_bytes=VMEM_LIMIT),
        interpret=INTERPRET,
    )(*pieces, *shards)
    return outs[:-2], outs[-2], outs[-1]


def per_device(
    tokens,
    lengths,
    page_table,
    attn_norm,
    qkv_weight,
    q_norm,
    k_norm,
    o_weight,
    mlp_norm,
    gate_up,
    down_weight,
):
    slots = tokens.shape[0]
    head_dim = q_norm.shape[0]
    local_kv = qkv_weight.shape[1]
    pages = page_table.shape[1]
    page_rows = slots // pages
    owned = slots // 4
    core = lax.axis_index("req") % 2
    z = lax.axis_index("mlp")

    units = gate_up.shape[0]
    padded = -(-units // 16) * 16
    pad = ((0, padded - units), (0, 0))
    own = jnp.concatenate(
        [jnp.pad(gate_up[:, 0, :], pad), jnp.pad(gate_up[:, 1, :], pad), jnp.pad(down_weight, pad)]
    )
    own1 = send(own, "xa", "xb")
    own2 = send(own, "xb", "xa")
    own3 = send(own1, "xb", "xa")
    chip_half = [own, own1, own2, own3]
    shards = chip_half + [send(w, "core", "core") for w in chip_half]

    first = jnp.where(core == 0, 1, 3)
    second = jnp.where(core == 0, 3, 1)
    normed = rms_scale(tokens.astype(f32), attn_norm).astype(bf16)
    qkv = jnp.einsum("sd,dkc->ksc", normed, qkv_weight, preferred_element_type=f32)
    context, pages_out = attention(
        qkv, q_norm, k_norm, lengths, page_table, jnp.stack([z, first, second])[None, :]
    )
    kv_cache = pages_out.reshape(2, local_kv, pages, page_rows, head_dim)
    kv_cache = kv_cache.transpose(0, 2, 3, 1, 4)

    def rows_of(values, owner):
        return lax.dynamic_slice_in_dim(values, owner * owned, owned, 0)

    out_leaving = jnp.dot(context[: 2 * owned], o_weight, preferred_element_type=f32).astype(bf16)
    arrived = send(out_leaving, "za", "zb").astype(f32)
    out_staying = jnp.dot(context[2 * owned :], o_weight, preferred_element_type=f32)
    out_staying = lax.optimization_barrier(out_staying) + arrived
    arrived = send(out_staying[owned:].astype(bf16), "zb", "za").astype(f32)
    attn_out = out_staying[:owned] + arrived
    resid = rows_of(tokens, z).astype(f32) + attn_out
    mlp_in = rms_scale(resid, mlp_norm).astype(bf16)

    half = owned // 2
    even, odd = [], []
    for i in range(2):
        mine = mlp_in[i * half : (i + 1) * half]
        even.append(mine)
        odd.append(cube_send(mine, i, 0))
    for step in (1, 2):
        for i in range(2):
            count = even[i].shape[0]
            came = cube_send(jnp.concatenate([even[i], odd[i]]), i, step)
            even[i] = jnp.concatenate([even[i], came[:count]])
            odd[i] = jnp.concatenate([odd[i], came[count:]])
    far_odd, far_even = [], []
    for i in range(2):
        far_odd.append(cube_send(odd[i], i, 3))
    for i in range(2):
        far_even.append(cube_send(even[i], i, 3))

    outs, gate_upper, down = feed_forward_first(odd + even, shards, (bf16, bf16, f32, f32))
    *odd_out, even0, even1 = outs
    even_out = [even0, even1]
    far_odd_out = feed_forward(far_odd, gate_upper, down, (bf16, bf16))
    far_even_out = feed_forward(far_even, gate_upper, down, (f32, f32))

    total = []
    for i in range(2):
        near = even_out[i] + cube_send(odd_out[i], i, 0).astype(f32)
        far = far_even_out[i] + cube_send(far_odd_out[i], i, 0).astype(f32)
        total.append(near + cube_send(far.astype(bf16), i, 3).astype(f32))
    for step in (2, 1):
        for i in range(2):
            rows = total[i].shape[0] // 2
            total[i] = total[i][:rows] + cube_send(total[i][rows:].astype(bf16), i, step).astype(f32)
    layer_out = (resid + jnp.concatenate(total)).astype(bf16)
    return (layer_out, kv_cache)


def solution(mesh):
    return jax.shard_map(
        per_device,
        mesh=mesh,
        in_specs=(
            P("req", None),
            P("req", None),
            P("req", None),
            P(),
            P(None, "mlp", None),
            P(),
            P(),
            P("mlp", None),
            P(),
            P(("req", "mlp"), None, None),
            P(("req", "mlp"), None),
        ),
        out_specs=(P(("req", "mlp"), None), P(None, "req", None, "mlp", None)),
        check_vma=False,
    )
```

```python
import math

import jax
import jax.numpy as jnp
from jax import lax
from jax.experimental import pallas as pl
from jax.experimental.pallas import tpu as pltpu
from jax.sharding import PartitionSpec as P


rope_theta = 1000000.0
norm_eps = 1e-06

AXES = ("req", "mlp")

bf16 = jnp.bfloat16
f32 = jnp.float32
VMEM_LIMIT = 16 * 2**20
INTERPRET = False
WHOLE = pl.BlockSpec(memory_space=pltpu.VMEM)

FLIPS = {
    "ya": (1, 0, 0, 0),
    "yb": (3, 0, 0, 0),
    "xa": (0, 1, 0, 0),
    "xb": (0, 3, 0, 0),
    "za": (0, 0, 0, 1),
    "zb": (0, 0, 0, 3),
    "core": (0, 0, 1, 0),
}
CUBE = ("ya", "za", "yb", "zb")


def pairs(flip_core0, flip_core1):
    out = []
    for y in range(4):
        for x in range(4):
            for core in range(2):
                for z in range(4):
                    fy, fx, fc, fz = FLIPS[flip_core1 if core else flip_core0]
                    there = (y ^ fy, x ^ fx, core ^ fc, z ^ fz)
                    src = ((y * 4 + x) * 2 + core) * 4 + z
                    dst = ((there[0] * 4 + there[1]) * 2 + there[2]) * 4 + there[3]
                    out.append((src, dst))
    return out


def send(values, flip_core0, flip_core1):
    return lax.ppermute(values, AXES, pairs(flip_core0, flip_core1))


def cube_send(values, slot, step):
    return send(values, CUBE[(slot + step) % 4], CUBE[(2 + slot + step) % 4])


def rms_scale(values, gain):
    mean_sq = jnp.mean(values * values, axis=-1, keepdims=True)
    return values * lax.rsqrt(mean_sq + norm_eps) * gain


def attention(qkv, q_norm, k_norm, lengths, page_table, place):
    local_kv, slots, _ = qkv.shape
    head_dim = q_norm.shape[0]
    half = head_dim // 2
    group_q = qkv.shape[2] // head_dim - 2
    prompts = lengths.shape[1]
    pages = page_table.shape[1]
    page_rows = slots // pages
    owned = slots // 4
    freq = rope_theta ** (-(2.0 * jnp.arange(half, dtype=f32)) / head_dim)
    freq = jnp.concatenate([freq, freq])[None, :]

    def kernel(lengths_ref, pages_ref, place_ref, qkv_ref, q_ref, k_ref, freq_ref, ctx_ref, kv_ref):
        def segments(dim, shape):
            ids = lax.broadcasted_iota(jnp.int32, shape, dim)
            segment = jnp.zeros(shape, jnp.int32)
            start = jnp.zeros(shape, jnp.int32)
            end = jnp.int32(0)
            for p in range(prompts):
                end = end + lengths_ref[0, p]
                segment = segment + (ids >= end).astype(jnp.int32)
                start = jnp.where(ids >= end, end, start)
            return ids, segment, ids - start

        _, _, position = segments(0, (slots, head_dim))
        angle = position.astype(f32) * freq_ref[...]
        cosine = jnp.cos(angle)
        sine = jnp.sin(angle)
        lane = lax.broadcasted_iota(jnp.int32, (slots, head_dim), 1)
        sine = jnp.where(lane < half, -sine, sine)
        query_id, query_segment, _ = segments(0, (slots, slots))
        key_id, key_segment, _ = segments(1, (slots, slots))
        allowed = (query_segment == key_segment) & (key_id <= query_id)

        def headed(values, gain):
            mean_sq = jnp.mean(values * values, axis=-1, keepdims=True)
            values = values * lax.rsqrt(mean_sq + norm_eps) * gain
            return (values * cosine + pltpu.roll(values, half, 1) * sine).astype(bf16)

        def block_at(owner):
            apart = owner ^ place_ref[0, 0]
            at = jnp.where(apart == place_ref[0, 1], 0, 1)
            at = jnp.where(apart == 0, 2, at)
            at = jnp.where(apart == place_ref[0, 2], 3, at)
            return pl.multiple_of(at * owned, owned)

        targets = [block_at(owner) for owner in range(4)]
        homes = [pl.multiple_of(pages_ref[0, p] * page_rows, page_rows) for p in range(pages)]
        for j in range(local_kv):
            key = headed(qkv_ref[j, :, group_q * head_dim : (group_q + 1) * head_dim], k_ref[...])
            value = qkv_ref[j, :, (group_q + 1) * head_dim :].astype(bf16)
            for p in range(pages):
                kv_ref[0, j, pl.ds(homes[p], page_rows), :] = key[p * page_rows : (p + 1) * page_rows]
                kv_ref[1, j, pl.ds(homes[p], page_rows), :] = value[
                    p * page_rows : (p + 1) * page_rows
                ]
            for i in range(group_q):
                query = headed(qkv_ref[j, :, i * head_dim : (i + 1) * head_dim], q_ref[...])
                scores = lax.dot_general(
                    query, key, (((1,), (1,)), ((), ())), preferred_element_type=f32
                ) * (1.0 / math.sqrt(head_dim))
                weights = jnp.where(allowed, jnp.exp(scores), 0.0)
                probs = (weights / jnp.sum(weights, axis=-1, keepdims=True)).astype(bf16)
                context = jnp.dot(probs, value, preferred_element_type=f32).astype(bf16)
                at = (j * group_q + i) * head_dim
                for owner in range(4):
                    ctx_ref[pl.ds(targets[owner], owned), at : at + head_dim] = context[
                        owner * owned : (owner + 1) * owned
                    ]

    scalars = pl.BlockSpec(memory_space=pltpu.SMEM)
    return pl.pallas_call(
        kernel,
        out_shape=[
            jax.ShapeDtypeStruct((slots, local_kv * group_q * head_dim), bf16),
            jax.ShapeDtypeStruct((2, local_kv, slots, head_dim), bf16),
        ],
        in_specs=[scalars] * 3 + [WHOLE] * 4,
        out_specs=[WHOLE] * 2,
        compiler_params=pltpu.CompilerParams(vmem_limit_bytes=VMEM_LIMIT),
        interpret=INTERPRET,
    )(lengths, page_table, place, qkv, q_norm[None, :], k_norm[None, :], freq)


def starts_of(pieces):
    return [sum(p.shape[0] for p in pieces[:i]) for i in range(len(pieces) + 1)]


def feed_forward_body(ins, rows, gate_upper_ref, down_ref, outs):
    starts = starts_of(ins)
    units = down_ref.shape[0]
    for i, piece in enumerate(ins):
        rows[starts[i] : starts[i + 1], :] = piece[...]
    hidden = lax.dot_general(
        rows[...], gate_upper_ref[...], (((1,), (1,)), ((), ())), preferred_element_type=f32
    )
    gate, upper = hidden[:, :units], hidden[:, units:]
    act = (gate / (1.0 + jnp.exp(-gate)) * upper).astype(bf16)
    out = jnp.dot(act, down_ref[...], preferred_element_type=f32)
    starts = starts_of(outs)
    for i, piece in enumerate(outs):
        piece[...] = out[starts[i] : starts[i + 1], :].astype(piece.dtype)


def feed_forward(pieces, gate_upper, down, outs):
    count = len(pieces)
    width = down.shape[1]

    def kernel(*refs):
        feed_forward_body(
            refs[:count], refs[-1], refs[count], refs[count + 1], refs[count + 2 : -1]
        )

    return pl.pallas_call(
        kernel,
        out_shape=[jax.ShapeDtypeStruct((r, width), t) for r, t in outs],
        in_specs=[WHOLE] * (count + 2),
        out_specs=[WHOLE] * len(outs),
        scratch_shapes=[pltpu.VMEM((starts_of(pieces)[-1], width), bf16)],
        compiler_params=pltpu.CompilerParams(vmem_limit_bytes=VMEM_LIMIT),
        interpret=INTERPRET,
    )(*pieces, gate_upper, down)


def feed_forward_first(pieces, shards, out_types):
    count, parts = len(pieces), len(shards)
    each = shards[0].shape[0] // 3
    width = shards[0].shape[1]
    units = parts * each

    def kernel(*refs):
        ins, held, outs = refs[:count], refs[count : count + parts], refs[count + parts : -3]
        gate_upper_ref, down_ref, rows = refs[-3:]
        for i, shard in enumerate(held):
            gate_upper_ref[i * each : (i + 1) * each, :] = shard[:each, :]
            gate_upper_ref[units + i * each : units + (i + 1) * each, :] = shard[each : 2 * each, :]
            down_ref[i * each : (i + 1) * each, :] = shard[2 * each :, :]
        feed_forward_body(ins, rows, gate_upper_ref, down_ref, outs)

    shapes = [jax.ShapeDtypeStruct(p.shape, t) for p, t in zip(pieces, out_types)]
    shapes.append(jax.ShapeDtypeStruct((2 * units, width), bf16))
    shapes.append(jax.ShapeDtypeStruct((units, width), bf16))
    outs = pl.pallas_call(
        kernel,
        out_shape=shapes,
        in_specs=[WHOLE] * (count + parts),
        out_specs=[WHOLE] * (count + 2),
        scratch_shapes=[pltpu.VMEM((starts_of(pieces)[-1], width), bf16)],
        compiler_params=pltpu.CompilerParams(vmem_limit_bytes=VMEM_LIMIT),
        interpret=INTERPRET,
    )(*pieces, *shards)
    return outs[:-2], outs[-2], outs[-1]


def per_device(
    tokens,
    lengths,
    page_table,
    attn_norm,
    qkv_weight,
    q_norm,
    k_norm,
    o_weight,
    mlp_norm,
    gate_up,
    down_weight,
):
    slots = tokens.shape[0]
    head_dim = q_norm.shape[0]
    local_kv = qkv_weight.shape[1]
    pages = page_table.shape[1]
    page_rows = slots // pages
    owned = slots // 4
    core = lax.axis_index("req") % 2
    z = lax.axis_index("mlp")

    units = gate_up.shape[0]
    padded = -(-units // 16) * 16
    pad = ((0, padded - units), (0, 0))
    own = jnp.concatenate(
        [jnp.pad(gate_up[:, 0, :], pad), jnp.pad(gate_up[:, 1, :], pad), jnp.pad(down_weight, pad)]
    )
    own1 = send(own, "xa", "xb")
    own2 = send(own, "xb", "xa")
    own3 = send(own1, "xb", "xa")
    chip_half = [own, own1, own2, own3]
    shards = list(chip_half)
    for held in chip_half:
        shards.append(send(held, "core", "core"))

    first = jnp.where(core == 0, 1, 3)
    second = jnp.where(core == 0, 3, 1)
    normed = rms_scale(tokens.astype(f32), attn_norm).astype(bf16)
    qkv = jnp.einsum("sd,dkc->ksc", normed, qkv_weight, preferred_element_type=f32)
    context, pages_out = attention(
        qkv, q_norm, k_norm, lengths, page_table, jnp.stack([z, first, second])[None, :]
    )
    kv_cache = pages_out.reshape(2, local_kv, pages, page_rows, head_dim)
    kv_cache = kv_cache.transpose(0, 2, 3, 1, 4)

    def rows_of(values, owner):
        return lax.dynamic_slice_in_dim(values, owner * owned, owned, 0)

    out_leaving = jnp.dot(context[: 2 * owned], o_weight, preferred_element_type=f32).astype(bf16)
    arrived = send(out_leaving, "za", "zb").astype(f32)
    out_staying = jnp.dot(context[2 * owned :], o_weight, preferred_element_type=f32)
    out_staying = lax.optimization_barrier(out_staying) + arrived
    arrived = send(out_staying[owned:].astype(bf16), "zb", "za").astype(f32)
    attn_out = out_staying[:owned] + arrived
    resid = rows_of(tokens, z).astype(f32) + attn_out
    mlp_in = rms_scale(resid, mlp_norm).astype(bf16)

    half = owned // 2
    even, odd = [], []
    for i in range(2):
        mine = mlp_in[i * half : (i + 1) * half]
        even.append(mine)
        odd.append(cube_send(mine, i, 0))
    for step in (1, 2):
        for i in range(2):
            count = even[i].shape[0]
            came = cube_send(jnp.concatenate([even[i], odd[i]]), i, step)
            even[i] = jnp.concatenate([even[i], came[:count]])
            odd[i] = jnp.concatenate([odd[i], came[count:]])
    far = []
    for i in range(2):
        far.append(cube_send(jnp.concatenate([odd[i], even[i]]), i, 3))

    outs, gate_upper, down = feed_forward_first(odd + even, shards, (bf16, bf16, f32, f32))
    *odd_out, even0, even1 = outs
    even_out = [even0, even1]
    far_odd_out, far_even_out = [], []
    for i in range(2):
        count = far[i].shape[0] // 2
        ins, outs = (far[i],), ((count, bf16), (count, f32))
        odd_part, even_part = feed_forward(ins, gate_upper, down, outs)
        far_odd_out.append(odd_part)
        far_even_out.append(even_part)

    total = []
    for i in range(2):
        near = even_out[i] + cube_send(odd_out[i], i, 0).astype(f32)
        across = far_even_out[i] + cube_send(far_odd_out[i], i, 0).astype(f32)
        total.append(near + cube_send(across.astype(bf16), i, 3).astype(f32))
    for step in (2, 1):
        for i in range(2):
            rows = total[i].shape[0] // 2
            total[i] = total[i][:rows] + cube_send(total[i][rows:].astype(bf16), i, step).astype(f32)
    layer_out = (resid + jnp.concatenate(total)).astype(bf16)
    return (layer_out, kv_cache)


def solution(mesh):
    return jax.shard_map(
        per_device,
        mesh=mesh,
        in_specs=(
            P("req", None),
            P("req", None),
            P("req", None),
            P(),
            P(None, "mlp", None),
            P(),
            P(),
            P("mlp", None),
            P(),
            P(("req", "mlp"), None, None),
            P(("req", "mlp"), None),
        ),
        out_specs=(P(("req", "mlp"), None), P(None, "req", None, "mlp", None)),
        check_vma=False,
    )
```

```python
import math

import jax
import jax.numpy as jnp
from jax import lax
from jax.experimental import pallas as pl
from jax.experimental.pallas import tpu as pltpu
from jax.sharding import PartitionSpec as P


rope_theta = 1000000.0
norm_eps = 1e-06

AXES = ("req", "mlp")

bf16 = jnp.bfloat16
f32 = jnp.float32
VMEM_LIMIT = 16 * 2**20
INTERPRET = False
WHOLE = pl.BlockSpec(memory_space=pltpu.VMEM)

FLIPS = {
    "ya": (1, 0, 0, 0),
    "yb": (3, 0, 0, 0),
    "xa": (0, 1, 0, 0),
    "xb": (0, 3, 0, 0),
    "za": (0, 0, 0, 1),
    "zb": (0, 0, 0, 3),
    "core": (0, 0, 1, 0),
}
CUBE = ("ya", "za", "yb", "zb")


def pairs(flip_core0, flip_core1):
    out = []
    for y in range(4):
        for x in range(4):
            for core in range(2):
                for z in range(4):
                    fy, fx, fc, fz = FLIPS[flip_core1 if core else flip_core0]
                    there = (y ^ fy, x ^ fx, core ^ fc, z ^ fz)
                    src = ((y * 4 + x) * 2 + core) * 4 + z
                    dst = ((there[0] * 4 + there[1]) * 2 + there[2]) * 4 + there[3]
                    out.append((src, dst))
    return out


def send(values, flip_core0, flip_core1):
    return lax.ppermute(values, AXES, pairs(flip_core0, flip_core1))


def cube_send(values, slot, step):
    return send(values, CUBE[(slot + step) % 4], CUBE[(2 + slot + step) % 4])


def rms_scale(values, gain):
    mean_sq = jnp.mean(values * values, axis=-1, keepdims=True)
    return values * lax.rsqrt(mean_sq + norm_eps) * gain


def attention(qkv, q_norm, k_norm, lengths, page_table, place):
    local_kv, slots, _ = qkv.shape
    head_dim = q_norm.shape[0]
    half = head_dim // 2
    group_q = qkv.shape[2] // head_dim - 2
    prompts = lengths.shape[1]
    pages = page_table.shape[1]
    page_rows = slots // pages
    owned = slots // 4
    freq = rope_theta ** (-(2.0 * jnp.arange(half, dtype=f32)) / head_dim)
    freq = jnp.concatenate([freq, freq])[None, :]

    def kernel(lengths_ref, pages_ref, place_ref, qkv_ref, q_ref, k_ref, freq_ref, ctx_ref, kv_ref):
        def segments(dim, shape):
            ids = lax.broadcasted_iota(jnp.int32, shape, dim)
            segment = jnp.zeros(shape, jnp.int32)
            start = jnp.zeros(shape, jnp.int32)
            end = jnp.int32(0)
            for p in range(prompts):
                end = end + lengths_ref[0, p]
                segment = segment + (ids >= end).astype(jnp.int32)
                start = jnp.where(ids >= end, end, start)
            return ids, segment, ids - start

        _, _, position = segments(0, (slots, head_dim))
        angle = position.astype(f32) * freq_ref[...]
        cosine = jnp.cos(angle)
        sine = jnp.sin(angle)
        lane = lax.broadcasted_iota(jnp.int32, (slots, head_dim), 1)
        sine = jnp.where(lane < half, -sine, sine)
        query_id, query_segment, _ = segments(0, (slots, slots))
        key_id, key_segment, _ = segments(1, (slots, slots))
        allowed = (query_segment == key_segment) & (key_id <= query_id)

        def headed(values, gain):
            mean_sq = jnp.mean(values * values, axis=-1, keepdims=True)
            values = values * lax.rsqrt(mean_sq + norm_eps) * gain
            return (values * cosine + pltpu.roll(values, half, 1) * sine).astype(bf16)

        def block_at(owner):
            apart = owner ^ place_ref[0, 0]
            at = jnp.where(apart == place_ref[0, 1], 0, 1)
            at = jnp.where(apart == 0, 2, at)
            at = jnp.where(apart == place_ref[0, 2], 3, at)
            return pl.multiple_of(at * owned, owned)

        targets = [block_at(owner) for owner in range(4)]
        homes = [pl.multiple_of(pages_ref[0, p] * page_rows, page_rows) for p in range(pages)]
        for j in range(local_kv):
            key = headed(qkv_ref[j, :, group_q * head_dim : (group_q + 1) * head_dim], k_ref[...])
            value = qkv_ref[j, :, (group_q + 1) * head_dim :].astype(bf16)
            for p in range(pages):
                kv_ref[0, j, pl.ds(homes[p], page_rows), :] = key[p * page_rows : (p + 1) * page_rows]
                kv_ref[1, j, pl.ds(homes[p], page_rows), :] = value[
                    p * page_rows : (p + 1) * page_rows
                ]
            for i in range(group_q):
                query = headed(qkv_ref[j, :, i * head_dim : (i + 1) * head_dim], q_ref[...])
                scores = lax.dot_general(
                    query, key, (((1,), (1,)), ((), ())), preferred_element_type=f32
                ) * (1.0 / math.sqrt(head_dim))
                weights = jnp.where(allowed, jnp.exp(scores), 0.0)
                probs = (weights / jnp.sum(weights, axis=-1, keepdims=True)).astype(bf16)
                context = jnp.dot(probs, value, preferred_element_type=f32).astype(bf16)
                at = (j * group_q + i) * head_dim
                for owner in range(4):
                    ctx_ref[pl.ds(targets[owner], owned), at : at + head_dim] = context[
                        owner * owned : (owner + 1) * owned
                    ]

    scalars = pl.BlockSpec(memory_space=pltpu.SMEM)
    return pl.pallas_call(
        kernel,
        out_shape=[
            jax.ShapeDtypeStruct((slots, local_kv * group_q * head_dim), bf16),
            jax.ShapeDtypeStruct((2, local_kv, slots, head_dim), bf16),
        ],
        in_specs=[scalars] * 3 + [WHOLE] * 4,
        out_specs=[WHOLE] * 2,
        compiler_params=pltpu.CompilerParams(vmem_limit_bytes=VMEM_LIMIT),
        interpret=INTERPRET,
    )(lengths, page_table, place, qkv, q_norm[None, :], k_norm[None, :], freq)


def starts_of(pieces):
    return [sum(p.shape[0] for p in pieces[:i]) for i in range(len(pieces) + 1)]


def feed_forward_body(ins, rows, gate_upper_ref, down_ref, outs):
    starts = starts_of(ins)
    units = down_ref.shape[0]
    for i, piece in enumerate(ins):
        rows[starts[i] : starts[i + 1], :] = piece[...]
    hidden = lax.dot_general(
        rows[...], gate_upper_ref[...], (((1,), (1,)), ((), ())), preferred_element_type=f32
    )
    gate, upper = hidden[:, :units], hidden[:, units:]
    act = (gate / (1.0 + jnp.exp(-gate)) * upper).astype(bf16)
    out = jnp.dot(act, down_ref[...], preferred_element_type=f32)
    starts = starts_of(outs)
    for i, piece in enumerate(outs):
        piece[...] = out[starts[i] : starts[i + 1], :].astype(piece.dtype)


def feed_forward(pieces, gate_upper, down, outs):
    count = len(pieces)
    width = down.shape[1]

    def kernel(*refs):
        feed_forward_body(
            refs[:count], refs[-1], refs[count], refs[count + 1], refs[count + 2 : -1]
        )

    return pl.pallas_call(
        kernel,
        out_shape=[jax.ShapeDtypeStruct((r, width), t) for r, t in outs],
        in_specs=[WHOLE] * (count + 2),
        out_specs=[WHOLE] * len(outs),
        scratch_shapes=[pltpu.VMEM((starts_of(pieces)[-1], width), bf16)],
        compiler_params=pltpu.CompilerParams(vmem_limit_bytes=VMEM_LIMIT),
        interpret=INTERPRET,
    )(*pieces, gate_upper, down)


def feed_forward_first(pieces, shards, out_types):
    count, parts = len(pieces), len(shards)
    each = shards[0].shape[0] // 3
    width = shards[0].shape[1]
    units = parts * each

    def kernel(*refs):
        ins, held, outs = refs[:count], refs[count : count + parts], refs[count + parts : -3]
        gate_upper_ref, down_ref, rows = refs[-3:]
        for i, shard in enumerate(held):
            gate_upper_ref[i * each : (i + 1) * each, :] = shard[:each, :]
            gate_upper_ref[units + i * each : units + (i + 1) * each, :] = shard[each : 2 * each, :]
            down_ref[i * each : (i + 1) * each, :] = shard[2 * each :, :]
        feed_forward_body(ins, rows, gate_upper_ref, down_ref, outs)

    shapes = [jax.ShapeDtypeStruct(p.shape, t) for p, t in zip(pieces, out_types)]
    shapes.append(jax.ShapeDtypeStruct((2 * units, width), bf16))
    shapes.append(jax.ShapeDtypeStruct((units, width), bf16))
    outs = pl.pallas_call(
        kernel,
        out_shape=shapes,
        in_specs=[WHOLE] * (count + parts),
        out_specs=[WHOLE] * (count + 2),
        scratch_shapes=[pltpu.VMEM((starts_of(pieces)[-1], width), bf16)],
        compiler_params=pltpu.CompilerParams(vmem_limit_bytes=VMEM_LIMIT),
        interpret=INTERPRET,
    )(*pieces, *shards)
    return outs[:-2], outs[-2], outs[-1]


def per_device(
    tokens,
    lengths,
    page_table,
    attn_norm,
    qkv_weight,
    q_norm,
    k_norm,
    o_weight,
    mlp_norm,
    gate_up,
    down_weight,
):
    slots = tokens.shape[0]
    head_dim = q_norm.shape[0]
    local_kv = qkv_weight.shape[1]
    pages = page_table.shape[1]
    page_rows = slots // pages
    owned = slots // 4
    core = lax.axis_index("req") % 2
    z = lax.axis_index("mlp")

    units = gate_up.shape[0]
    padded = -(-units // 16) * 16
    pad = ((0, padded - units), (0, 0))
    own = jnp.concatenate(
        [jnp.pad(gate_up[:, 0, :], pad), jnp.pad(gate_up[:, 1, :], pad), jnp.pad(down_weight, pad)]
    )
    own1 = send(own, "xa", "xb")
    own2 = send(own, "xb", "xa")
    own3 = send(own1, "xb", "xa")
    chip_half = [own, own1, own2, own3]
    shards = list(chip_half)
    for held in chip_half:
        shards.append(send(held, "core", "core"))

    first = jnp.where(core == 0, 1, 3)
    second = jnp.where(core == 0, 3, 1)
    normed = rms_scale(tokens.astype(f32), attn_norm).astype(bf16)
    qkv = jnp.einsum("sd,dkc->ksc", normed, qkv_weight, preferred_element_type=f32)
    context, pages_out = attention(
        qkv, q_norm, k_norm, lengths, page_table, jnp.stack([z, first, second])[None, :]
    )
    kv_cache = pages_out.reshape(2, local_kv, pages, page_rows, head_dim)
    kv_cache = kv_cache.transpose(0, 2, 3, 1, 4)

    def rows_of(values, owner):
        return lax.dynamic_slice_in_dim(values, owner * owned, owned, 0)

    out_leaving = jnp.dot(context[: 2 * owned], o_weight, preferred_element_type=f32).astype(bf16)
    arrived = send(out_leaving, "za", "zb").astype(f32)
    out_staying = jnp.dot(context[2 * owned :], o_weight, preferred_element_type=f32)
    out_staying = lax.optimization_barrier(out_staying) + arrived
    arrived = send(out_staying[owned:].astype(bf16), "zb", "za").astype(f32)
    attn_out = out_staying[:owned] + arrived
    resid = rows_of(tokens, z).astype(f32) + attn_out
    mlp_in = rms_scale(resid, mlp_norm).astype(bf16)

    half = owned // 2
    even, odd = [], []
    for i in range(2):
        mine = mlp_in[i * half : (i + 1) * half]
        even.append(mine)
        odd.append(cube_send(mine, i, 0))
    for step in (1, 2):
        for i in range(2):
            count = even[i].shape[0]
            came = cube_send(jnp.concatenate([even[i], odd[i]]), i, step)
            even[i] = jnp.concatenate([even[i], came[:count]])
            odd[i] = jnp.concatenate([odd[i], came[count:]])
    far_odd, far_even = [], []
    for i in range(2):
        far_odd.append(cube_send(odd[i], i, 3))
    for i in range(2):
        far_even.append(cube_send(even[i], i, 3))

    outs, gate_upper, down = feed_forward_first(odd + even, shards, (bf16, bf16, f32, f32))
    *odd_out, even0, even1 = outs
    even_out = [even0, even1]
    count = far_odd[0].shape[0]
    far_odd_out = feed_forward(far_odd, gate_upper, down, ((count, bf16), (count, bf16)))
    far_even_out = feed_forward(far_even, gate_upper, down, ((count, f32), (count, f32)))

    total = []
    for i in range(2):
        near = even_out[i] + cube_send(odd_out[i], i, 0).astype(f32)
        across = far_even_out[i] + cube_send(far_odd_out[i], i, 0).astype(f32)
        total.append(near + cube_send(across.astype(bf16), i, 3).astype(f32))
    for step in (2, 1):
        for i in range(2):
            rows = total[i].shape[0] // 2
            total[i] = total[i][:rows] + cube_send(total[i][rows:].astype(bf16), i, step).astype(f32)
    layer_out = (resid + jnp.concatenate(total)).astype(bf16)
    return (layer_out, kv_cache)


def solution(mesh):
    return jax.shard_map(
        per_device,
        mesh=mesh,
        in_specs=(
            P("req", None),
            P("req", None),
            P("req", None),
            P(),
            P(None, "mlp", None),
            P(),
            P(),
            P("mlp", None),
            P(),
            P(("req", "mlp"), None, None),
            P(("req", "mlp"), None),
        ),
        out_specs=(P(("req", "mlp"), None), P(None, "req", None, "mlp", None)),
        check_vma=False,
    )
```
